32 devices in a mesh: blk: 4 (over y, x), hid: 8 (over z, core).
Axes of the slice: x: 2, y: 2, z: 4, core: 2. Of those that a mesh axis runs over, the one named last changes fastest.
Arguments:
- images: bfloat16 [8192, 1024], P(('blk', 'hid')), may hold values from -0.1875 to 0.1875
- caption_ids: int32 [8192], P(('blk', 'hid')), may hold values from 0 to 2047, as said below
- captions: bfloat16 [2048, 1024], P(('blk', 'hid')), may hold values from -0.75 to 0.75
- caption_feats: bfloat16 [2048, 1024], P(('blk', 'hid')), may hold values from -1.5 to 1.5
- w_in: bfloat16 [1024, 32768], P('blk', 'hid'), may hold values from -0.1875 to 0.1875
- w_out: bfloat16 [1024, 32768], P('blk', 'hid'), may hold values from -0.03125 to 0.03125
- logit_scale: float32 [1], replicated, may hold values from 8 to 16
- logit_bias: float32 [1], replicated, may hold values from -3 to -1
Outputs:
- image_grad: bfloat16 [8192, 1024], P(('blk', 'hid'))
- feat_grad: bfloat16 [2048, 1024], P(('blk', 'hid'))
- w_in_grad: bfloat16 [1024, 32768], P('blk', 'hid')
- w_out_grad: bfloat16 [1024, 32768], P('blk', 'hid')
The draws below stay inside these ranges and needn't reach their ends.
Inputs may be any that keep to these rules, and one draw needn't show every extreme that they name: `caption_ids`: the image rows of block b name caption rows of the caption blocks b, b - 1, ..., b - 2 (mod the number of blocks); the first image row of every block names the last caption row of its own block, the second names the first.
All inputs are finite; a program needn't handle non-finite values.
Results may differ from the reference program's by a relative error of at most 0.019.
Values may be sent and summed in bfloat16 or wider, within the bound.
A program may use at most 128 MiB of HBM per device.

```python
import math
import jax
import jax.numpy as jnp
from jax import lax

D = 1024
FF = 32768
IMG_DEV = 256
CAP_DEV = 64
HOPS = 2
IMAGES = 8192
CAPTIONS = 2048
GROUP_ROWS = 512
N_BLK = 4
N_HID = 8


def draw_caption_ids(key, part):
    devices = N_BLK * N_HID
    key_hop, key_row = jax.random.split(jax.random.fold_in(key, 17))
    hops = jax.random.randint(key_hop, (devices, IMG_DEV), 0, HOPS + 1, dtype=jnp.int32)
    rows = jax.random.randint(key_row, (devices, IMG_DEV), 0, CAP_DEV, dtype=jnp.int32)
    column = jnp.arange(IMG_DEV, dtype=jnp.int32)[None, :]
    hops = jnp.where(column < 2, 0, hops)
    rows = jnp.where(column == 0, CAP_DEV - 1, jnp.where(column == 1, 0, rows))
    blocks = (jnp.arange(devices, dtype=jnp.int32)[:, None] - hops) % devices
    return (blocks * CAP_DEV + rows).reshape(-1).astype(jnp.int32)


def block_scale(own_key, dims, shards, low, top_value):
    gain = 1.0
    for dim, shards_of in shards:
        heights = jax.random.uniform(jax.random.fold_in(jax.random.fold_in(own_key, 6), dim), (shards_of,), jnp.float32, low / len(shards), top_value / len(shards))
        gain = gain * jnp.repeat(jnp.exp(heights), dims[dim] // shards_of).reshape((-1,) + (1,) * (len(dims) - 1 - dim))
    return gain


def bell_draw(stream_key, dims, deviation, limit, cuts=(), kind=jnp.bfloat16):
    drawn = jax.random.normal(stream_key, dims, jnp.float32) * deviation
    if len(cuts) > 0:
        drawn = block_scale(stream_key, dims, cuts, -0.22, 0.18) * drawn
    return jnp.clip(drawn, min=-limit, max=limit).astype(kind)


def setup_inputs(seed: int = 0) -> dict:
    streams_of = jax.random.split(jax.random.key(seed), 9)
    images = bell_draw(streams_of[0], (IMAGES, D), 0.03, 0.1875, ((0, 32),))
    caption_ids = draw_caption_ids(jax.random.fold_in(streams_of[8], 71), 0)
    captions = bell_draw(streams_of[2], (CAPTIONS, D), 0.125, 0.75, ((0, 32),))
    caption_feats = bell_draw(streams_of[3], (CAPTIONS, D), 0.25, 1.5, ((0, 32),))
    w_in = bell_draw(streams_of[4], (D, FF), D ** -0.5, 0.1875, ((0, 4), (1, 8)))
    w_out = bell_draw(streams_of[5], (D, FF), FF ** -0.5, 0.03125, ((0, 4), (1, 8)))
    logit_scale = jnp.clip(jnp.exp(jax.random.uniform(streams_of[6], (1,), jnp.float32, math.log(8.0), math.log(16.0))), 8.0, 16.0)
    logit_bias = jnp.clip(jax.random.uniform(streams_of[7], (1,), jnp.float32, -3.0, -1.0), -3.0, -1.0)
    return {"images": images, "caption_ids": caption_ids, "captions": captions, "caption_feats": caption_feats, "w_in": w_in, "w_out": w_out, "logit_scale": logit_scale, "logit_bias": logit_bias}


def gelu_parts(values):
    coefficient = math.sqrt(2.0 / math.pi)
    inner_arg = coefficient * (values + 0.044715 * values * values * values)
    tangent = jnp.tanh(inner_arg)
    output = 0.5 * values * (1.0 + tangent)
    gelu_slope = 0.5 * (1.0 + tangent) + 0.5 * values * (1.0 - tangent * tangent) * coefficient * (1.0 + 3.0 * 0.044715 * values * values)
    return (output, gelu_slope)

def contract(left_side, right_side, left_dim, right_dim):
    return lax.dot_general(left_side, right_side, (((left_dim,), (right_dim,)), ((), ())), preferred_element_type=jnp.float32)

def reference(images, caption_ids, captions, caption_feats, w_in, w_out, logit_scale, logit_bias):
    devices = N_BLK * N_HID
    temper = logit_scale[0]
    offset = logit_bias[0]
    image_blocks = images.reshape(devices, IMG_DEV, D)
    id_blocks = caption_ids.reshape(devices, IMG_DEV)
    cap_blocks = captions.reshape(devices, CAP_DEV, D)
    owners = jnp.arange(devices, dtype=jnp.int32)
    cap_local = jnp.arange(CAP_DEV, dtype=jnp.int32)

    def one_device(inputs):
        image_rows, id_rows, device = inputs
        image_acc = jnp.zeros((IMG_DEV, D), jnp.float32)
        hop_terms = []
        for stride in range(HOPS + 1):
            holder = ((device - stride) % devices).astype(jnp.int32)
            current = lax.dynamic_index_in_dim(cap_blocks, holder, 0, keepdims=False)
            logits = temper * contract(current, image_rows, 1, 1) + offset
            global_rows = holder * CAP_DEV + cap_local
            positive = (global_rows[:, None] == id_rows[None, :]).astype(jnp.float32)
            pair_grad = (jax.nn.sigmoid(logits) - positive).astype(jnp.bfloat16)
            image_acc = image_acc + contract(pair_grad, current, 0, 0)
            hop_terms.append(temper * jnp.dot(pair_grad, image_rows, preferred_element_type=jnp.float32))
        return ((temper * image_acc).astype(jnp.bfloat16), jnp.stack(hop_terms))
    image_out, term_blocks = lax.map(one_device, (image_blocks, id_blocks, owners))
    cap_acc = term_blocks[:, 0]
    for stride in range(1, HOPS + 1):
        cap_acc = cap_acc + jnp.roll(term_blocks[:, stride], -stride, axis=0)
    caption_grad = cap_acc.reshape(CAPTIONS, D)
    caption_round = caption_grad.astype(jnp.bfloat16)
    grad_groups = caption_round.reshape(N_BLK, GROUP_ROWS, D)
    feat_groups = caption_feats.reshape(N_BLK, GROUP_ROWS, D)

    def group_step(totals, pair):
        grad_rows, feat_rows = pair
        pre_act = jnp.dot(feat_rows, w_in, preferred_element_type=jnp.float32)
        act_grad = jnp.dot(grad_rows, w_out, preferred_element_type=jnp.float32)
        output, gelu_slope = gelu_parts(pre_act)
        active = output.astype(jnp.bfloat16)
        pre_grad = (act_grad * gelu_slope).astype(jnp.bfloat16)
        in_part = lax.optimization_barrier(contract(feat_rows, pre_grad, 0, 0).astype(jnp.bfloat16)).astype(jnp.float32)
        out_part = lax.optimization_barrier(contract(grad_rows, active, 0, 0).astype(jnp.bfloat16)).astype(jnp.float32)
        branch = contract(pre_grad, w_in, 1, 1)
        return ((totals[0] + in_part, totals[1] + out_part), branch)
    zero_init = jnp.zeros((D, FF), jnp.float32)
    sums, branches = lax.scan(group_step, (zero_init, zero_init), (grad_groups, feat_groups))
    feat_grad = (caption_grad + branches.reshape(CAPTIONS, D)).astype(jnp.bfloat16)
    return (image_out.reshape(IMAGES, D), feat_grad, sums[0].astype(jnp.bfloat16), sums[1].astype(jnp.bfloat16))
```

```python
import math

import jax
import jax.numpy as jnp
from jax import lax
from jax.sharding import PartitionSpec as P

HOPS = 2


def from_behind(shard, axis, by):
    length = lax.axis_size(axis)
    return lax.ppermute(shard, axis, [(i, (i + by) % length) for i in range(length)])


def gelu_parts(values):
    coefficient = math.sqrt(2.0 / math.pi)
    inner_arg = coefficient * (values + 0.044715 * values * values * values)
    tangent = jnp.tanh(inner_arg)
    output = 0.5 * values * (1.0 + tangent)
    gelu_slope = 0.5 * (1.0 + tangent) + 0.5 * values * (1.0 - tangent * tangent) * coefficient * (
        1.0 + 3.0 * 0.044715 * values * values
    )
    return (output, gelu_slope)


def contract(left_side, right_side, left_dim, right_dim):
    return lax.dot_general(
        left_side,
        right_side,
        (((left_dim,), (right_dim,)), ((), ())),
        preferred_element_type=jnp.float32,
    )


def shards(images, caption_ids, captions, caption_feats, w_in, w_out, logit_scale, logit_bias):
    temper = logit_scale[0]
    offset = logit_bias[0]
    cap_rows = captions.shape[0]
    devices = lax.axis_size(("blk", "hid"))
    device = lax.axis_index(("blk", "hid"))
    cap_local = lax.broadcasted_iota(jnp.int32, (cap_rows, 1), 0)
    image_acc = jnp.zeros(images.shape, jnp.float32)
    current = captions
    carried = None
    own_grad = None
    for stride in range(HOPS + 1):
        if stride > 0:
            current = from_behind(current, ("blk", "hid"), 1)
        holder = (device - stride) % devices
        global_rows = holder * cap_rows + cap_local
        positive = (global_rows == caption_ids[None, :]).astype(jnp.float32)
        logits = temper * contract(current, images, 1, 1) + offset
        pair_grad = (jax.nn.sigmoid(logits) - positive).astype(jnp.bfloat16)
        image_acc = image_acc + contract(pair_grad, current, 0, 0)
        hop_term = temper * jnp.dot(pair_grad, images, preferred_element_type=jnp.float32)
        if stride > 0:
            carried = (
                from_behind(carried.astype(jnp.bfloat16), ("blk", "hid"), 1).astype(carried.dtype)
                + hop_term
            )
        else:
            carried = hop_term
    own_grad = from_behind(carried.astype(jnp.bfloat16), ("blk", "hid"), -HOPS).astype(
        carried.dtype
    )
    image_grad = (temper * image_acc).astype(jnp.bfloat16)
    caption_round = own_grad.astype(jnp.bfloat16)
    both = ("blk", "hid")
    feats_all = lax.all_gather(caption_feats, both, axis=0, tiled=True)
    full_in = lax.all_to_all(w_in, "blk", 1, 0, tiled=True)
    full_out = lax.all_to_all(w_out, "blk", 1, 0, tiled=True)
    rows_all = lax.all_gather(caption_round, both, axis=0, tiled=True)
    pre_act = jnp.dot(feats_all, full_in, preferred_element_type=jnp.float32)
    act_grad = jnp.dot(rows_all, full_out, preferred_element_type=jnp.float32)
    output, gelu_slope = gelu_parts(pre_act)
    active = output.astype(jnp.bfloat16)
    pre_grad = (act_grad * gelu_slope).astype(jnp.bfloat16)
    part = contract(pre_grad, full_in, 1, 1).astype(jnp.bfloat16)
    part = lax.psum_scatter(part, "blk", scatter_dimension=0, tiled=True)
    part = lax.psum_scatter(part, "hid", scatter_dimension=0, tiled=True)
    branch = part.astype(jnp.float32)
    w_in_grad = lax.all_to_all(
        contract(feats_all, pre_grad, 0, 0).astype(jnp.bfloat16), "blk", 0, 1, tiled=True
    )
    w_out_grad = lax.all_to_all(
        contract(rows_all, active, 0, 0).astype(jnp.bfloat16), "blk", 0, 1, tiled=True
    )
    feat_grad = (own_grad + branch).astype(jnp.bfloat16)
    return (image_grad, feat_grad, w_in_grad, w_out_grad)


def solution(mesh):
    return jax.shard_map(
        shards,
        mesh=mesh,
        in_specs=(
            P(("blk", "hid"), None),
            P(("blk", "hid")),
            P(("blk", "hid"), None),
            P(("blk", "hid"), None),
            P("blk", "hid"),
            P("blk", "hid"),
            P(),
            P(),
        ),
        out_specs=(
            P(("blk", "hid"), None),
            P(("blk", "hid"), None),
            P("blk", "hid"),
            P("blk", "hid"),
        ),
        check_vma=False,
    )
```

```python
import functools
import math

import jax
import jax.numpy as jnp
from jax import lax
from jax.experimental import pallas as pl
from jax.experimental.pallas import tpu as pltpu
from jax.sharding import PartitionSpec as P

HOPS = 2


def from_behind(shard, axis, by):
    length = lax.axis_size(axis)
    return lax.ppermute(shard, axis, [(i, (i + by) % length) for i in range(length)])


def gelu_parts(values):
    coefficient = math.sqrt(2.0 / math.pi)
    inner_arg = coefficient * (values + 0.044715 * values * values * values)
    tangent = jnp.tanh(inner_arg)
    output = 0.5 * values * (1.0 + tangent)
    gelu_slope = 0.5 * (1.0 + tangent) + 0.5 * values * (1.0 - tangent * tangent) * coefficient * (
        1.0 + 3.0 * 0.044715 * values * values
    )
    return (output, gelu_slope)


def contract(left_side, right_side, left_dim, right_dim):
    return lax.dot_general(
        left_side,
        right_side,
        (((left_dim,), (right_dim,)), ((), ())),
        preferred_element_type=jnp.float32,
    )


def spread_kernel(n_blk, n_hid, rows_ref, win_ref, wout_ref, all_ref, fin_ref, fout_ref,
                  keep_in, keep_out, local_sem, w_send, w_recv,
                  a_send, a_recv, b_send, b_recv, c_send, c_recv):
    blk = lax.axis_index("blk")
    hid = lax.axis_index("hid")
    pairs = n_hid // 2
    core = lax.rem(hid, 2)
    place = lax.div(hid, 2)
    cap = rows_ref.shape[0]
    depth = win_ref.shape[0]
    width = fin_ref.shape[1]
    mesh_id = pl.DeviceIdType.MESH

    def peer_blk(step):
        return lax.rem(blk + step, n_blk)

    def peer_place(step):
        return lax.rem(place + step, pairs)

    def rows_of(block, spot, side):
        start = ((block * pairs + spot) * 2 + side) * cap
        return pl.ds(pl.multiple_of(start, cap), cap)

    partner = (blk, place * 2 + 1 - core)
    barrier = pltpu.get_barrier_semaphore()
    for step in range(1, n_blk):
        pl.semaphore_signal(barrier, inc=1, device_id=(peer_blk(step), hid), device_id_type=mesh_id)
    for step in range(1, pairs):
        pl.semaphore_signal(
            barrier, inc=1, device_id=(blk, peer_place(step) * 2 + core), device_id_type=mesh_id
        )
    pl.semaphore_signal(barrier, inc=1, device_id=partner, device_id_type=mesh_id)
    pl.semaphore_wait(barrier, n_blk + pairs - 1)

    started = []

    def send(src, dst, send_sem, recv_sem, device):
        copy = pltpu.make_async_remote_copy(
            src_ref=src, dst_ref=dst, send_sem=send_sem, recv_sem=recv_sem,
            device_id=device, device_id_type=mesh_id,
        )
        copy.start()
        started.append(copy)
        return copy

    own = rows_of(blk, place, core)
    along = []
    for step in range(1, pairs):
        along.append(send(rows_ref, all_ref.at[own], a_send.at[step - 1], a_recv.at[step - 1],
                          (blk, peer_place(step) * 2 + core)))
    across = {}
    for step in range(1, n_blk):
        across[(step, 0)] = send(rows_ref, all_ref.at[own], b_send.at[step - 1, 0],
                                 b_recv.at[step - 1, 0], (peer_blk(step), hid))
    twin = [send(rows_ref, all_ref.at[own], c_send.at[0, 0], c_recv.at[0, 0], partner)]
    locals_ = [pltpu.make_async_copy(rows_ref, all_ref.at[own], local_sem.at[0])]
    mine = pl.ds(pl.multiple_of(blk * width, width), width)
    takes = [
        pltpu.make_async_copy(win_ref.at[:, mine], keep_in, local_sem.at[1]),
        pltpu.make_async_copy(wout_ref.at[:, mine], keep_out, local_sem.at[2]),
    ]
    for copy in locals_ + takes:
        copy.start()
    band = pl.ds(pl.multiple_of(blk * depth, depth), depth)
    weights = []

    def send_weight(which, src_ref, dst_ref):
        for step in range(1, n_blk):
            other = pl.ds(pl.multiple_of(peer_blk(step) * width, width), width)
            weights.append(send(src_ref.at[:, other], dst_ref.at[band, :],
                                w_send.at[which, step - 1], w_recv.at[which, step - 1],
                                (peer_blk(step), hid)))

    for step in range(1, pairs):
        along[step - 1].wait_recv()
        got = rows_of(blk, lax.rem(place + pairs - step, pairs), core)
        for far in range(1, n_blk):
            across[(far, step)] = send(all_ref.at[got], all_ref.at[got], b_send.at[far - 1, step],
                                       b_recv.at[far - 1, step], (peer_blk(far), hid))
        twin.append(send(all_ref.at[got], all_ref.at[got], c_send.at[0, step],
                         c_recv.at[0, step], partner))
    send_weight(0, win_ref, fin_ref)
    send_weight(1, wout_ref, fout_ref)
    puts = [
        pltpu.make_async_copy(keep_in, fin_ref.at[band, :], local_sem.at[3]),
        pltpu.make_async_copy(keep_out, fout_ref.at[band, :], local_sem.at[4]),
    ]
    for take, put in zip(takes, puts):
        take.wait()
        put.start()
    for step in range(pairs):
        spot = lax.rem(place + pairs - step, pairs)
        for far in range(1, n_blk):
            across[(far, step)].wait_recv()
            got = rows_of(lax.rem(blk + n_blk - far, n_blk), spot, core)
            twin.append(send(all_ref.at[got], all_ref.at[got], c_send.at[far, step],
                             c_recv.at[far, step], partner))
    for copy in weights + twin:
        copy.wait_recv()
    for copy in started:
        copy.wait_send()
    for copy in locals_ + puts:
        copy.wait()


def spread(rows, w_in, w_out):
    n_blk, n_hid = lax.axis_size("blk"), lax.axis_size("hid")
    depth, hidden = w_in.shape
    width = hidden // n_blk
    pairs = n_hid // 2
    dma = pltpu.SemaphoreType.DMA
    near = max(pairs - 1, 1)
    full = jax.ShapeDtypeStruct((depth * n_blk, width), w_in.dtype)
    return pl.pallas_call(
        functools.partial(spread_kernel, n_blk, n_hid),
        out_shape=(
            jax.ShapeDtypeStruct((rows.shape[0] * n_blk * n_hid, rows.shape[1]), rows.dtype),
            full,
            full,
        ),
        in_specs=[
            pl.BlockSpec(memory_space=pltpu.VMEM),
            pl.BlockSpec(memory_space=pl.ANY),
            pl.BlockSpec(memory_space=pl.ANY),
        ],
        out_specs=[pl.BlockSpec(memory_space=pl.ANY)] * 3,
        scratch_shapes=[
            pltpu.VMEM((depth, width), w_in.dtype),
            pltpu.VMEM((depth, width), w_in.dtype),
            dma((5,)),
            dma((2, n_blk - 1)), dma((2, n_blk - 1)),
            dma((near,)), dma((near,)),
            dma((n_blk - 1, pairs)), dma((n_blk - 1, pairs)),
            dma((n_blk, pairs)), dma((n_blk, pairs)),
        ],
        compiler_params=pltpu.CompilerParams(collective_id=0, has_side_effects=True),
    )(rows, w_in, w_out)


def fold_rows(part):
    n_blk, n_hid = lax.axis_size("blk"), lax.axis_size("hid")
    pairs = n_hid // 2
    hid = lax.axis_index("hid")
    core, place = hid % 2, hid // 2
    parts = part.reshape(n_blk, pairs, 2, -1, part.shape[1])
    give = lax.dynamic_index_in_dim(parts, 1 - core, 2, keepdims=False)
    keep = lax.dynamic_index_in_dim(parts, core, 2, keepdims=False)
    came = lax.ppermute(give, "hid", [(i, i ^ 1) for i in range(n_hid)])
    both = (keep.astype(jnp.float32) + came.astype(jnp.float32)).astype(part.dtype)
    spread_out = lax.all_to_all(both, "blk", 0, 0, tiled=True)
    mine = jnp.sum(spread_out.astype(jnp.float32), axis=0).astype(part.dtype)
    total = lax.dynamic_index_in_dim(mine, place, 0, keepdims=False).astype(jnp.float32)
    for step in range(1, pairs):
        piece = lax.dynamic_index_in_dim(mine, (place + step) % pairs, 0, keepdims=False)
        moves = [(i, (i + 2 * step) % n_hid) for i in range(n_hid)]
        total = total + lax.ppermute(piece, "hid", moves).astype(jnp.float32)
    return total


def shards(images, caption_ids, captions, caption_feats, w_in, w_out, logit_scale, logit_bias):
    temper = logit_scale[0]
    offset = logit_bias[0]
    cap_rows = captions.shape[0]
    devices = lax.axis_size(("blk", "hid"))
    device = lax.axis_index(("blk", "hid"))
    cap_local = lax.broadcasted_iota(jnp.int32, (cap_rows, 1), 0)
    image_acc = jnp.zeros(images.shape, jnp.float32)
    current = captions
    carried = None
    own_grad = None
    for stride in range(HOPS + 1):
        if stride > 0:
            current = from_behind(current, ("blk", "hid"), 1)
        holder = (device - stride) % devices
        global_rows = holder * cap_rows + cap_local
        positive = (global_rows == caption_ids[None, :]).astype(jnp.float32)
        logits = temper * contract(current, images, 1, 1) + offset
        pair_grad = (jax.nn.sigmoid(logits) - positive).astype(jnp.bfloat16)
        image_acc = image_acc + contract(pair_grad, current, 0, 0)
        hop_term = temper * jnp.dot(pair_grad, images, preferred_element_type=jnp.float32)
        if stride > 0:
            carried = (
                from_behind(carried.astype(jnp.bfloat16), ("blk", "hid"), 1).astype(carried.dtype)
                + hop_term
            )
        else:
            carried = hop_term
    own_grad = from_behind(carried.astype(jnp.bfloat16), ("blk", "hid"), -HOPS).astype(
        carried.dtype
    )
    image_grad = (temper * image_acc).astype(jnp.bfloat16)
    caption_round = own_grad.astype(jnp.bfloat16)
    both = ("blk", "hid")
    feats_all = lax.all_gather(caption_feats, both, axis=0, tiled=True)
    rows_all, full_in, full_out = spread(caption_round, w_in, w_out)
    pre_act = jnp.dot(feats_all, full_in, preferred_element_type=jnp.float32)
    act_grad = jnp.dot(rows_all, full_out, preferred_element_type=jnp.float32)
    output, gelu_slope = gelu_parts(pre_act)
    active = output.astype(jnp.bfloat16)
    pre_grad = (act_grad * gelu_slope).astype(jnp.bfloat16)
    part = contract(pre_grad, full_in, 1, 1).astype(jnp.bfloat16)
    branch = fold_rows(part)
    w_in_grad = lax.all_to_all(
        contract(feats_all, pre_grad, 0, 0).astype(jnp.bfloat16), "blk", 0, 1, tiled=True
    )
    w_out_grad = lax.all_to_all(
        contract(rows_all, active, 0, 0).astype(jnp.bfloat16), "blk", 0, 1, tiled=True
    )
    feat_grad = (own_grad + branch).astype(jnp.bfloat16)
    return (image_grad, feat_grad, w_in_grad, w_out_grad)


def solution(mesh):
    return jax.shard_map(
        shards,
        mesh=mesh,
        in_specs=(
            P(("blk", "hid"), None),
            P(("blk", "hid")),
            P(("blk", "hid"), None),
            P(("blk", "hid"), None),
            P("blk", "hid"),
            P("blk", "hid"),
            P(),
            P(),
        ),
        out_specs=(
            P(("blk", "hid"), None),
            P(("blk", "hid"), None),
            P("blk", "hid"),
            P("blk", "hid"),
        ),
        check_vma=False,
    )
```

```python
import functools
import math

import jax
import jax.numpy as jnp
from jax import lax
from jax.experimental import pallas as pl
from jax.experimental.pallas import tpu as pltpu
from jax.sharding import PartitionSpec as P

HOPS = 2


def from_behind(shard, axis, by):
    length = lax.axis_size(axis)
    return lax.ppermute(shard, axis, [(i, (i + by) % length) for i in range(length)])


def gelu_parts(values):
    coefficient = math.sqrt(2.0 / math.pi)
    inner_arg = coefficient * (values + 0.044715 * values * values * values)
    tangent = jnp.tanh(inner_arg)
    output = 0.5 * values * (1.0 + tangent)
    gelu_slope = 0.5 * (1.0 + tangent) + 0.5 * values * (1.0 - tangent * tangent) * coefficient * (
        1.0 + 3.0 * 0.044715 * values * values
    )
    return (output, gelu_slope)


def contract(left_side, right_side, left_dim, right_dim):
    return lax.dot_general(
        left_side,
        right_side,
        (((left_dim,), (right_dim,)), ((), ())),
        preferred_element_type=jnp.float32,
    )


def spread_kernel(n_blk, n_hid, rows_ref, wout_ref, all_ref, fout_ref,
                  keep_out, local_sem, w_send, w_recv,
                  a_send, a_recv, b_send, b_recv, c_send, c_recv):
    blk = lax.axis_index("blk")
    hid = lax.axis_index("hid")
    pairs = n_hid // 2
    core = lax.rem(hid, 2)
    place = lax.div(hid, 2)
    cap = rows_ref.shape[0]
    depth = wout_ref.shape[0]
    width = fout_ref.shape[1]
    mesh_id = pl.DeviceIdType.MESH

    def peer_blk(step):
        return lax.rem(blk + step, n_blk)

    def peer_place(step):
        return lax.rem(place + step, pairs)

    def rows_of(block, spot, side):
        start = ((block * pairs + spot) * 2 + side) * cap
        return pl.ds(pl.multiple_of(start, cap), cap)

    partner = (blk, place * 2 + 1 - core)
    barrier = pltpu.get_barrier_semaphore()
    for step in range(1, n_blk):
        pl.semaphore_signal(barrier, inc=1, device_id=(peer_blk(step), hid), device_id_type=mesh_id)
    for step in range(1, pairs):
        pl.semaphore_signal(
            barrier, inc=1, device_id=(blk, peer_place(step) * 2 + core), device_id_type=mesh_id
        )
    pl.semaphore_signal(barrier, inc=1, device_id=partner, device_id_type=mesh_id)
    pl.semaphore_wait(barrier, n_blk + pairs - 1)

    started = []

    def send(src, dst, send_sem, recv_sem, device):
        copy = pltpu.make_async_remote_copy(
            src_ref=src, dst_ref=dst, send_sem=send_sem, recv_sem=recv_sem,
            device_id=device, device_id_type=mesh_id,
        )
        copy.start()
        started.append(copy)
        return copy

    own = rows_of(blk, place, core)
    along = []
    for step in range(1, pairs):
        along.append(send(rows_ref, all_ref.at[own], a_send.at[step - 1], a_recv.at[step - 1],
                          (blk, peer_place(step) * 2 + core)))
    across = {}
    for step in range(1, n_blk):
        across[(step, 0)] = send(rows_ref, all_ref.at[own], b_send.at[step - 1, 0],
                                 b_recv.at[step - 1, 0], (peer_blk(step), hid))
    twin = [send(rows_ref, all_ref.at[own], c_send.at[0, 0], c_recv.at[0, 0], partner)]
    locals_ = [pltpu.make_async_copy(rows_ref, all_ref.at[own], local_sem.at[0])]
    mine = pl.ds(pl.multiple_of(blk * width, width), width)
    takes = [
        pltpu.make_async_copy(wout_ref.at[:, mine], keep_out, local_sem.at[2]),
    ]
    for copy in locals_ + takes:
        copy.start()
    band = pl.ds(pl.multiple_of(blk * depth, depth), depth)
    weights = []

    def send_weight(which, src_ref, dst_ref):
        for step in range(1, n_blk):
            other = pl.ds(pl.multiple_of(peer_blk(step) * width, width), width)
            weights.append(send(src_ref.at[:, other], dst_ref.at[band, :],
                                w_send.at[which, step - 1], w_recv.at[which, step - 1],
                                (peer_blk(step), hid)))

    for step in range(1, pairs):
        along[step - 1].wait_recv()
        got = rows_of(blk, lax.rem(place + pairs - step, pairs), core)
        for far in range(1, n_blk):
            across[(far, step)] = send(all_ref.at[got], all_ref.at[got], b_send.at[far - 1, step],
                                       b_recv.at[far - 1, step], (peer_blk(far), hid))
        twin.append(send(all_ref.at[got], all_ref.at[got], c_send.at[0, step],
                         c_recv.at[0, step], partner))
    send_weight(0, wout_ref, fout_ref)
    puts = [
        pltpu.make_async_copy(keep_out, fout_ref.at[band, :], local_sem.at[1]),
    ]
    for take, put in zip(takes, puts):
        take.wait()
        put.start()
    for step in range(pairs):
        spot = lax.rem(place + pairs - step, pairs)
        for far in range(1, n_blk):
            across[(far, step)].wait_recv()
            got = rows_of(lax.rem(blk + n_blk - far, n_blk), spot, core)
            twin.append(send(all_ref.at[got], all_ref.at[got], c_send.at[far, step],
                             c_recv.at[far, step], partner))
    for copy in weights + twin:
        copy.wait_recv()
    for copy in started:
        copy.wait_send()
    for copy in locals_ + puts:
        copy.wait()


def spread(rows, w_out):
    n_blk, n_hid = lax.axis_size("blk"), lax.axis_size("hid")
    depth, hidden = w_out.shape
    width = hidden // n_blk
    pairs = n_hid // 2
    dma = pltpu.SemaphoreType.DMA
    near = max(pairs - 1, 1)
    full = jax.ShapeDtypeStruct((depth * n_blk, width), w_out.dtype)
    return pl.pallas_call(
        functools.partial(spread_kernel, n_blk, n_hid),
        out_shape=(
            jax.ShapeDtypeStruct((rows.shape[0] * n_blk * n_hid, rows.shape[1]), rows.dtype),
            full,
        ),
        in_specs=[
            pl.BlockSpec(memory_space=pltpu.VMEM),
            pl.BlockSpec(memory_space=pl.ANY),
        ],
        out_specs=[pl.BlockSpec(memory_space=pl.ANY)] * 2,
        scratch_shapes=[
            pltpu.VMEM((depth, width), w_out.dtype),
            dma((3,)),
            dma((1, n_blk - 1)), dma((1, n_blk - 1)),
            dma((near,)), dma((near,)),
            dma((n_blk - 1, pairs)), dma((n_blk - 1, pairs)),
            dma((n_blk, pairs)), dma((n_blk, pairs)),
        ],
        compiler_params=pltpu.CompilerParams(collective_id=0, has_side_effects=True),
    )(rows, w_out)


def fold_rows(part, ahead, behind):
    n_blk, n_hid = lax.axis_size("blk"), lax.axis_size("hid")
    pairs = n_hid // 2
    hid = lax.axis_index("hid")
    core, place = hid % 2, hid // 2
    parts = part.reshape(n_blk, pairs, 2, -1, part.shape[1])
    give = lax.dynamic_index_in_dim(parts, 1 - core, 2, keepdims=False)
    keep = lax.dynamic_index_in_dim(parts, core, 2, keepdims=False)
    came = lax.ppermute(give, "hid", [(i, i ^ 1) for i in range(n_hid)])
    both = (keep.astype(jnp.float32) + came.astype(jnp.float32)).astype(part.dtype)
    both, ahead = lax.optimization_barrier((both, ahead))
    spread_out = lax.all_to_all(both, "blk", 0, 0, tiled=True)
    spread_out, behind = lax.optimization_barrier((spread_out, behind))
    mine = jnp.sum(spread_out.astype(jnp.float32), axis=0).astype(part.dtype)
    total = lax.dynamic_index_in_dim(mine, place, 0, keepdims=False).astype(jnp.float32)
    for step in range(1, pairs):
        piece = lax.dynamic_index_in_dim(mine, (place + step) % pairs, 0, keepdims=False)
        moves = [(i, (i + 2 * step) % n_hid) for i in range(n_hid)]
        total = total + lax.ppermute(piece, "hid", moves).astype(jnp.float32)
    return total, ahead, behind


def work(images, caption_ids, captions, caption_feats, w_in, w_out, logit_scale, logit_bias):
    temper = logit_scale[0]
    offset = logit_bias[0]
    cap_rows = captions.shape[0]
    devices = lax.axis_size(("blk", "hid"))
    device = lax.axis_index(("blk", "hid"))
    cap_local = lax.broadcasted_iota(jnp.int32, (cap_rows, 1), 0)
    image_acc = jnp.zeros(images.shape, jnp.float32)
    current = captions
    carried = None
    own_grad = None
    for stride in range(HOPS + 1):
        if stride > 0:
            current = from_behind(current, ("blk", "hid"), 1)
        holder = (device - stride) % devices
        global_rows = holder * cap_rows + cap_local
        positive = (global_rows == caption_ids[None, :]).astype(jnp.float32)
        logits = temper * contract(current, images, 1, 1) + offset
        pair_grad = (jax.nn.sigmoid(logits) - positive).astype(jnp.bfloat16)
        image_acc = image_acc + contract(pair_grad, current, 0, 0)
        hop_term = temper * jnp.dot(pair_grad, images, preferred_element_type=jnp.float32)
        if stride > 0:
            carried = (
                from_behind(carried.astype(jnp.bfloat16), ("blk", "hid"), 1).astype(carried.dtype)
                + hop_term
            )
        else:
            carried = hop_term
    own_grad = from_behind(carried.astype(jnp.bfloat16), ("blk", "hid"), -HOPS).astype(
        carried.dtype
    )
    image_grad = (temper * image_acc).astype(jnp.bfloat16)
    caption_round = own_grad.astype(jnp.bfloat16)
    both = ("blk", "hid")
    feats_all = lax.all_gather(caption_feats, both, axis=0, tiled=True)
    full_in = lax.all_to_all(w_in, "blk", 1, 0, tiled=True)
    rows_all, full_out = spread(caption_round, w_out)
    pre_act = jnp.dot(feats_all, full_in, preferred_element_type=jnp.float32)
    output = gelu_parts(pre_act)[0]
    active = output.astype(jnp.bfloat16)
    out_part = contract(rows_all, active, 0, 0).astype(jnp.bfloat16)
    out_part, rows_later, pre_later = lax.optimization_barrier((out_part, rows_all, pre_act))
    w_out_grad = lax.all_to_all(out_part, "blk", 0, 1, tiled=True)
    act_grad = jnp.dot(rows_later, full_out, preferred_element_type=jnp.float32)
    pre_grad = (act_grad * gelu_parts(pre_later)[1]).astype(jnp.bfloat16)
    in_part = contract(feats_all, pre_grad, 0, 0).astype(jnp.bfloat16)
    part = contract(pre_grad, full_in, 1, 1).astype(jnp.bfloat16)
    branch, w_out_grad, in_part = fold_rows(part, w_out_grad, in_part)
    w_in_grad = lax.all_to_all(in_part, "blk", 0, 1, tiled=True)
    feat_grad = (own_grad + branch).astype(jnp.bfloat16)
    return (image_grad, feat_grad, w_in_grad, w_out_grad)


def solution(mesh):
    return jax.shard_map(
        work,
        mesh=mesh,
        in_specs=(
            P(("blk", "hid"), None),
            P(("blk", "hid")),
            P(("blk", "hid"), None),
            P(("blk", "hid"), None),
            P("blk", "hid"),
            P("blk", "hid"),
            P(),
            P(),
        ),
        out_specs=(
            P(("blk", "hid"), None),
            P(("blk", "hid"), None),
            P("blk", "hid"),
            P("blk", "hid"),
        ),
        check_vma=False,
    )
```

```python
import functools
import math

import jax
import jax.numpy as jnp
from jax import lax
from jax.experimental import pallas as pl
from jax.experimental.pallas import tpu as pltpu
from jax.experimental.layout import Layout, with_layout_constraint
from jax.sharding import PartitionSpec as P

HOPS = 2


def from_behind(shard, axis, by):
    length = lax.axis_size(axis)
    return lax.ppermute(shard, axis, [(i, (i + by) % length) for i in range(length)])


def gelu_parts(values):
    coefficient = math.sqrt(2.0 / math.pi)
    inner_arg = coefficient * (values + 0.044715 * values * values * values)
    tangent = jnp.tanh(inner_arg)
    output = 0.5 * values * (1.0 + tangent)
    gelu_slope = 0.5 * (1.0 + tangent) + 0.5 * values * (1.0 - tangent * tangent) * coefficient * (
        1.0 + 3.0 * 0.044715 * values * values
    )
    return (output, gelu_slope)


def contract(left_side, right_side, left_dim, right_dim):
    return lax.dot_general(
        left_side,
        right_side,
        (((left_dim,), (right_dim,)), ((), ())),
        preferred_element_type=jnp.float32,
    )


def spread_kernel(n_blk, n_hid, rows_ref, wout_ref, all_ref, fout_ref,
                  keep_out, local_sem, w_send, w_recv,
                  a_send, a_recv, b_send, b_recv, c_send, c_recv):
    blk = lax.axis_index("blk")
    hid = lax.axis_index("hid")
    pairs = n_hid // 2
    core = lax.rem(hid, 2)
    place = lax.div(hid, 2)
    cap = rows_ref.shape[0]
    depth = wout_ref.shape[0]
    width = fout_ref.shape[1]
    mesh_id = pl.DeviceIdType.MESH

    def peer_blk(step):
        return lax.rem(blk + step, n_blk)

    def peer_place(step):
        return lax.rem(place + step, pairs)

    def rows_of(block, spot, side):
        start = ((block * pairs + spot) * 2 + side) * cap
        return pl.ds(pl.multiple_of(start, cap), cap)

    partner = (blk, place * 2 + 1 - core)
    barrier = pltpu.get_barrier_semaphore()
    for step in range(1, n_blk):
        pl.semaphore_signal(barrier, inc=1, device_id=(peer_blk(step), hid), device_id_type=mesh_id)
    for step in range(1, pairs):
        pl.semaphore_signal(
            barrier, inc=1, device_id=(blk, peer_place(step) * 2 + core), device_id_type=mesh_id
        )
    pl.semaphore_signal(barrier, inc=1, device_id=partner, device_id_type=mesh_id)
    pl.semaphore_wait(barrier, n_blk + pairs - 1)

    started = []

    def send(src, dst, send_sem, recv_sem, device):
        copy = pltpu.make_async_remote_copy(
            src_ref=src, dst_ref=dst, send_sem=send_sem, recv_sem=recv_sem,
            device_id=device, device_id_type=mesh_id,
        )
        copy.start()
        started.append(copy)
        return copy

    own = rows_of(blk, place, core)
    along = []
    for step in range(1, pairs):
        along.append(send(rows_ref, all_ref.at[own], a_send.at[step - 1], a_recv.at[step - 1],
                          (blk, peer_place(step) * 2 + core)))
    across = {}
    for step in range(1, n_blk):
        across[(step, 0)] = send(rows_ref, all_ref.at[own], b_send.at[step - 1, 0],
                                 b_recv.at[step - 1, 0], (peer_blk(step), hid))
    twin = [send(rows_ref, all_ref.at[own], c_send.at[0, 0], c_recv.at[0, 0], partner)]
    locals_ = [pltpu.make_async_copy(rows_ref, all_ref.at[own], local_sem.at[0])]
    mine = pl.ds(pl.multiple_of(blk * width, width), width)
    takes = [
        pltpu.make_async_copy(wout_ref.at[:, mine], keep_out, local_sem.at[2]),
    ]
    for copy in locals_ + takes:
        copy.start()
    band = pl.ds(pl.multiple_of(blk * depth, depth), depth)
    weights = []

    def send_weight(which, src_ref, dst_ref):
        for step in range(1, n_blk):
            other = pl.ds(pl.multiple_of(peer_blk(step) * width, width), width)
            weights.append(send(src_ref.at[:, other], dst_ref.at[band, :],
                                w_send.at[which, step - 1], w_recv.at[which, step - 1],
                                (peer_blk(step), hid)))

    for step in range(1, pairs):
        along[step - 1].wait_recv()
        got = rows_of(blk, lax.rem(place + pairs - step, pairs), core)
        for far in range(1, n_blk):
            across[(far, step)] = send(all_ref.at[got], all_ref.at[got], b_send.at[far - 1, step],
                                       b_recv.at[far - 1, step], (peer_blk(far), hid))
        twin.append(send(all_ref.at[got], all_ref.at[got], c_send.at[0, step],
                         c_recv.at[0, step], partner))
    send_weight(0, wout_ref, fout_ref)
    puts = [
        pltpu.make_async_copy(keep_out, fout_ref.at[band, :], local_sem.at[1]),
    ]
    for take, put in zip(takes, puts):
        take.wait()
        put.start()
    for step in range(pairs):
        spot = lax.rem(place + pairs - step, pairs)
        for far in range(1, n_blk):
            across[(far, step)].wait_recv()
            got = rows_of(lax.rem(blk + n_blk - far, n_blk), spot, core)
            twin.append(send(all_ref.at[got], all_ref.at[got], c_send.at[far, step],
                             c_recv.at[far, step], partner))
    for copy in weights + twin:
        copy.wait_recv()
    for copy in started:
        copy.wait_send()
    for copy in locals_ + puts:
        copy.wait()


def spread(rows, w_out):
    n_blk, n_hid = lax.axis_size("blk"), lax.axis_size("hid")
    depth, hidden = w_out.shape
    width = hidden // n_blk
    pairs = n_hid // 2
    dma = pltpu.SemaphoreType.DMA
    near = max(pairs - 1, 1)
    full = jax.ShapeDtypeStruct((depth * n_blk, width), w_out.dtype)
    return pl.pallas_call(
        functools.partial(spread_kernel, n_blk, n_hid),
        out_shape=(
            jax.ShapeDtypeStruct((rows.shape[0] * n_blk * n_hid, rows.shape[1]), rows.dtype),
            full,
        ),
        in_specs=[
            pl.BlockSpec(memory_space=pltpu.VMEM),
            pl.BlockSpec(memory_space=pl.ANY),
        ],
        out_specs=[pl.BlockSpec(memory_space=pl.ANY)] * 2,
        scratch_shapes=[
            pltpu.VMEM((depth, width), w_out.dtype),
            dma((3,)),
            dma((1, n_blk - 1)), dma((1, n_blk - 1)),
            dma((near,)), dma((near,)),
            dma((n_blk - 1, pairs)), dma((n_blk - 1, pairs)),
            dma((n_blk, pairs)), dma((n_blk, pairs)),
        ],
        compiler_params=pltpu.CompilerParams(collective_id=0, has_side_effects=True),
    )(rows, w_out)


def fold_rows(part, ahead, behind):
    n_blk, n_hid = lax.axis_size("blk"), lax.axis_size("hid")
    pairs = n_hid // 2
    hid = lax.axis_index("hid")
    core, place = hid % 2, hid // 2
    parts = part.reshape(n_blk, pairs, 2, -1, part.shape[1])
    give = lax.dynamic_index_in_dim(parts, 1 - core, 2, keepdims=False)
    keep = lax.dynamic_index_in_dim(parts, core, 2, keepdims=False)
    came = lax.ppermute(give, "hid", [(i, i ^ 1) for i in range(n_hid)])
    both = (keep.astype(jnp.float32) + came.astype(jnp.float32)).astype(part.dtype)
    both, ahead = lax.optimization_barrier((both, ahead))
    spread_out = lax.all_to_all(both, "blk", 0, 0, tiled=True)
    spread_out, behind = lax.optimization_barrier((spread_out, behind))
    mine = jnp.sum(spread_out.astype(jnp.float32), axis=0).astype(part.dtype)
    total = lax.dynamic_index_in_dim(mine, place, 0, keepdims=False).astype(jnp.float32)
    for step in range(1, pairs):
        piece = lax.dynamic_index_in_dim(mine, (place + step) % pairs, 0, keepdims=False)
        moves = [(i, (i + 2 * step) % n_hid) for i in range(n_hid)]
        total = total + lax.ppermute(piece, "hid", moves).astype(jnp.float32)
    return total, ahead, behind


def work(images, caption_ids, captions, caption_feats, w_in, w_out, logit_scale, logit_bias):
    temper = logit_scale[0]
    offset = logit_bias[0]
    cap_rows = captions.shape[0]
    devices = lax.axis_size(("blk", "hid"))
    device = lax.axis_index(("blk", "hid"))
    cap_local = lax.broadcasted_iota(jnp.int32, (cap_rows, 1), 0)
    image_acc = jnp.zeros(images.shape, jnp.float32)
    current = captions
    carried = None
    own_grad = None
    for stride in range(HOPS + 1):
        if stride > 0:
            current = from_behind(current, ("blk", "hid"), 1)
        holder = (device - stride) % devices
        global_rows = holder * cap_rows + cap_local
        positive = (global_rows == caption_ids[None, :]).astype(jnp.float32)
        logits = temper * contract(current, images, 1, 1) + offset
        pair_grad = (jax.nn.sigmoid(logits) - positive).astype(jnp.bfloat16)
        image_acc = image_acc + contract(pair_grad, current, 0, 0)
        hop_term = temper * jnp.dot(pair_grad, images, preferred_element_type=jnp.float32)
        if stride > 0:
            carried = (
                from_behind(carried.astype(jnp.bfloat16), ("blk", "hid"), 1).astype(carried.dtype)
                + hop_term
            )
        else:
            carried = hop_term
    own_grad = from_behind(carried.astype(jnp.bfloat16), ("blk", "hid"), -HOPS).astype(
        carried.dtype
    )
    image_grad = (temper * image_acc).astype(jnp.bfloat16)
    caption_round = own_grad.astype(jnp.bfloat16)
    both = ("blk", "hid")
    feats_all = lax.all_gather(caption_feats, both, axis=0, tiled=True)
    n_blk = lax.axis_size("blk")
    cut = w_in.reshape(w_in.shape[0], n_blk, -1).transpose(1, 0, 2)
    cut = with_layout_constraint(cut, Layout((0, 1, 2)))
    full_in = lax.all_to_all(cut, "blk", 0, 0, tiled=True).reshape(-1, cut.shape[2])
    rows_all, full_out = spread(caption_round, w_out)
    pre_act = jnp.dot(feats_all, full_in, preferred_element_type=jnp.float32)
    output = gelu_parts(pre_act)[0]
    active = output.astype(jnp.bfloat16)
    out_part = contract(rows_all, active, 0, 0).astype(jnp.bfloat16)
    out_part, rows_later, pre_later = lax.optimization_barrier((out_part, rows_all, pre_act))
    w_out_grad = lax.all_to_all(out_part, "blk", 0, 1, tiled=True)
    act_grad = jnp.dot(rows_later, full_out, preferred_element_type=jnp.float32)
    pre_grad = (act_grad * gelu_parts(pre_later)[1]).astype(jnp.bfloat16)
    in_part = contract(feats_all, pre_grad, 0, 0).astype(jnp.bfloat16)
    in_part = with_layout_constraint(in_part, Layout((0, 1)))
    part = contract(pre_grad, full_in, 1, 1).astype(jnp.bfloat16)
    branch, w_out_grad, in_part = fold_rows(part, w_out_grad, in_part)
    w_in_grad = lax.all_to_all(in_part, "blk", 0, 1, tiled=True)
    feat_grad = (own_grad + branch).astype(jnp.bfloat16)
    return (image_grad, feat_grad, w_in_grad, w_out_grad)


def solution(mesh):
    return jax.shard_map(
        work,
        mesh=mesh,
        in_specs=(
            P(("blk", "hid"), None),
            P(("blk", "hid")),
            P(("blk", "hid"), None),
            P(("blk", "hid"), None),
            P("blk", "hid"),
            P("blk", "hid"),
            P(),
            P(),
        ),
        out_specs=(
            P(("blk", "hid"), None),
            P(("blk", "hid"), None),
            P("blk", "hid"),
            P("blk", "hid"),
        ),
        check_vma=False,
    )
```
